32 devices in a mesh: shard: 2 (over y), ctx: 4 (over x, core), tp: 4 (over z).
Axes of the slice: x: 2, y: 2, z: 4, core: 2. Of those that a mesh axis runs over, the one named last changes fastest.
Arguments:
- tokens: bfloat16 [2, 1024, 1024], P('shard', 'ctx'), may hold values from -6 to 6
- cotangent: bfloat16 [2, 1024, 1024], P('shard', 'ctx'), may hold values from -6 to 6
- block_order: int32 [8], replicated, may hold values from 0 to 7, as said below
- attn_gain: bfloat16 [1024], P('shard'), may hold values from 0.25 to 1.75
- w_query: bfloat16 [1024, 2048], P('shard', 'tp'), may hold values from -0.1875 to 0.1875
- key_weight: bfloat16 [1024, 1024], P('shard', 'tp'), may hold values from -0.1875 to 0.1875
- value_weight: bfloat16 [1024, 1024], P('shard', 'tp'), may hold values from -0.1875 to 0.1875
- w_out: bfloat16 [2048, 1024], P('tp', 'shard'), may hold values from -2 to 2
- query_gain: bfloat16 [128], P('shard'), may hold values from 0.6 to 3.6
- key_gain: bfloat16 [128], P('shard'), may hold values from 0.6 to 3.6
- mlp_gain: bfloat16 [1024], P('shard'), may hold values from 0.25 to 1.75
- w_gate: bfloat16 [1024, 3072], P('shard', 'tp'), may hold values from -0.1875 to 0.1875
- w_up: bfloat16 [1024, 3072], P('shard', 'tp'), may hold values from -0.1875 to 0.1875
- w_down: bfloat16 [3072, 1024], P('tp', 'shard'), may hold values from -0.109375 to 0.109375
Outputs:
- layer_out: bfloat16 [2, 1024, 1024], P('shard', 'ctx')
- tokens_grad: float32 [2, 1024, 1024], P('shard', 'ctx')
- attn_gain_grad: float32 [1024], P('shard')
- w_query_grad: float32 [1024, 2048], P('shard', 'tp')
- w_key_grad: float32 [1024, 1024], P('shard', 'tp')
- w_value_grad: float32 [1024, 1024], P('shard', 'tp')
- w_out_grad: float32 [2048, 1024], P('tp', 'shard')
- query_gain_grad: float32 [128], P('shard')
- key_gain_grad: float32 [128], P('shard')
- mlp_gain_grad: float32 [1024], P('shard')
- w_gate_grad: float32 [1024, 3072], P('shard', 'tp')
- w_up_grad: float32 [1024, 3072], P('shard', 'tp')
- w_down_grad: float32 [3072, 1024], P('tp', 'shard')
The draws below stay inside these ranges and needn't reach their ends.
Inputs may be any that keep to these rules, and one draw needn't show every extreme that they name: Stored block j of every sequence holds the tokens at positions block_order[j] * 128 to (block_order[j] + 1) * 128 - 1, in order; block_order is a permutation in which stored blocks 2 c and 2 c + 1 hold position blocks b and 7 - b for some b, in either order.
All inputs are finite; a program needn't handle non-finite values.
Results may differ from the reference program's by a relative error of at most 0.029.
The reference program's roundings to bfloat16 on the way count: a program that leaves them out, or rounds other values in their place, can miss the bound.
Values may be sent and summed in bfloat16 or wider, within the bound.
No kernel may reach another device: no remote copies, remote signals or barrier semaphores. Data moves between devices by JAX's collectives and lax.ppermute only.
A program may use at most 128 MiB of HBM per device.

```python
import jax
import jax.numpy as jnp
from jax import lax

MODEL_WIDTH = 1024
QUERY_HEADS = 16
KEY_VALUE_HEADS = 8
HEAD_SIZE = 128
FF = 3072
BLKLEN = 128
NBLK = 8
SEQUENCE_TOKENS = 1024
SEQS = 2


def draw_block_order(key, part):
    pair_key = jax.random.fold_in(key, 37)
    flip_key = jax.random.fold_in(key, 41)
    half_count = NBLK // 2
    pairs = jax.random.permutation(pair_key, half_count).astype(jnp.int32)
    flips = jax.random.randint(flip_key, (half_count,), 0, 2).astype(jnp.int32)
    first = jnp.where(flips == 1, NBLK - 1 - pairs, pairs).astype(jnp.int32)
    second = (NBLK - 1 - first).astype(jnp.int32)
    return jnp.stack([first, second], axis=1).reshape(NBLK).astype(jnp.int32)


def draw_query_gain(key, part):
    subkey = jax.random.fold_in(key, 11)
    values = jax.random.uniform(subkey, (HEAD_SIZE,), jnp.float32, 0.6, 1.4)
    return values.astype(jnp.bfloat16)


def draw_key_gain(key, part):
    subkey = jax.random.fold_in(key, 23)
    values = jax.random.uniform(subkey, (HEAD_SIZE,), jnp.float32, 0.6, 1.4)
    return values.astype(jnp.bfloat16)


def steps_of(stream_key, shape, cuts, smallest, high):
    gain, own = 1.0, jax.random.fold_in(stream_key, 6)
    for dim, shards_of in cuts:
        draws = jnp.exp(jax.random.uniform(jax.random.fold_in(own, dim), (shards_of,), jnp.float32, smallest / len(cuts), high / len(cuts)))
        gain = gain * jnp.repeat(draws, shape[dim] // shards_of).reshape([-1 if axis == dim else 1 for axis in range(len(shape))])
    return gain


def centred(own_key, extent, deviation, bound, cuts=(), kind=jnp.bfloat16):
    drawn = deviation * jax.random.normal(own_key, extent, jnp.float32)
    if cuts:
        drawn = drawn * steps_of(own_key, extent, cuts, -0.22, 0.18)
    return jnp.clip(drawn, -bound, bound).astype(kind)


def setup_inputs(seed: int = 0) -> dict:
    streams_of = jax.random.split(jax.random.key(seed), 15)
    tokens = centred(streams_of[0], (SEQS, SEQUENCE_TOKENS, MODEL_WIDTH), 1.0, 6.0, ((0, 2), (1, 4)))
    cotangent = centred(streams_of[1], (SEQS, SEQUENCE_TOKENS, MODEL_WIDTH), 1.0, 6.0, ((0, 2), (1, 4)))
    block_order = draw_block_order(jax.random.fold_in(streams_of[14], 71), 0)
    attn_gain = jnp.clip(1.0 + 0.15 * jax.random.normal(streams_of[3], (MODEL_WIDTH,), jnp.float32), 0.25, 1.75).astype(jnp.bfloat16)
    w_query = centred(streams_of[4], (MODEL_WIDTH, QUERY_HEADS * HEAD_SIZE), MODEL_WIDTH ** -0.5, 0.1875, ((0, 2), (1, 4)))
    key_weight = centred(streams_of[5], (MODEL_WIDTH, KEY_VALUE_HEADS * HEAD_SIZE), MODEL_WIDTH ** -0.5, 0.1875, ((0, 2), (1, 4)))
    value_weight = centred(streams_of[6], (MODEL_WIDTH, KEY_VALUE_HEADS * HEAD_SIZE), MODEL_WIDTH ** -0.5, 0.1875, ((0, 2), (1, 4)))
    w_out = centred(streams_of[7], (QUERY_HEADS * HEAD_SIZE, MODEL_WIDTH), (max(1, QUERY_HEADS * HEAD_SIZE // (2 * BLKLEN))) ** -0.5, 2.0, ((0, 4), (1, 2)))
    query_gain = draw_query_gain(jax.random.fold_in(streams_of[14], 71), 0)
    key_gain = draw_key_gain(jax.random.fold_in(streams_of[14], 71), 0)
    mlp_gain = jnp.clip(1.0 + 0.15 * jax.random.normal(streams_of[10], (MODEL_WIDTH,), jnp.float32), 0.25, 1.75).astype(jnp.bfloat16)
    w_gate = centred(streams_of[11], (MODEL_WIDTH, FF), MODEL_WIDTH ** -0.5, 0.1875, ((0, 2), (1, 4)))
    w_up = centred(streams_of[12], (MODEL_WIDTH, FF), MODEL_WIDTH ** -0.5, 0.1875, ((0, 2), (1, 4)))
    w_down = centred(streams_of[13], (FF, MODEL_WIDTH), FF ** -0.5, 0.109375, ((0, 4), (1, 2)))
    return {"tokens": tokens, "cotangent": cotangent, "block_order": block_order, "attn_gain": attn_gain, "w_query": w_query, "key_weight": key_weight, "value_weight": value_weight, "w_out": w_out, "query_gain": query_gain, "key_gain": key_gain, "mlp_gain": mlp_gain, "w_gate": w_gate, "w_up": w_up, "w_down": w_down}


EPSILON = 1e-06
THETA = 1000000.0
NEG_LARGE = -1e+30

def matrix_product(left_op, right_op):
    return jnp.dot(left_op, right_op, preferred_element_type=jnp.float32)

def normalize(values):
    inverse = lax.rsqrt(lax.optimization_barrier(jnp.mean(values * values, axis=-1, keepdims=True)) + EPSILON)
    return (values * inverse, inverse)

def normalize_backward(grad_in, normed, inverse, gain_row):
    scaled = grad_in * gain_row
    return inverse * (scaled - normed * lax.optimization_barrier(jnp.mean(scaled * normed, axis=-1, keepdims=True)))

def rope_tables(token_pos):
    half_width = HEAD_SIZE // 2
    frequency = 1.0 / THETA ** (jnp.arange(half_width, dtype=jnp.float32) * 2.0 / HEAD_SIZE)
    angles = token_pos.astype(jnp.float32)[:, None] * frequency[None, :]
    return (jnp.cos(angles)[:, None, :], jnp.sin(angles)[:, None, :])

def rotate(values, cosine, sine_table):
    half_width = values.shape[-1] // 2
    first_half = values[..., :half_width]
    second_half = values[..., half_width:]
    return jnp.concatenate([first_half * cosine - second_half * sine_table, second_half * cosine + first_half * sine_table], axis=-1)

def rotate_back(values, cosine, sine_table):
    half_width = values.shape[-1] // 2
    first_half = values[..., :half_width]
    second_half = values[..., half_width:]
    return jnp.concatenate([first_half * cosine + second_half * sine_table, second_half * cosine - first_half * sine_table], axis=-1)

def attention_head(query_rows, key_rows, value_rows, allowed, head_scale):
    scores = jnp.dot(query_rows, key_rows.T, preferred_element_type=jnp.float32) * head_scale
    scores = jnp.where(allowed, scores, NEG_LARGE)
    row_best = lax.optimization_barrier(jnp.max(scores, axis=-1, keepdims=True))
    weights = jnp.where(allowed, jnp.exp(scores - row_best), 0.0)
    row_total = lax.optimization_barrier(jnp.sum(weights, axis=-1, keepdims=True))
    output = jnp.dot(weights.astype(jnp.bfloat16), value_rows, preferred_element_type=jnp.float32) / row_total
    return (output, row_best[:, 0] + jnp.log(row_total[:, 0]))

def attention_head_back(query_rows, key_rows, value_rows, allowed, log_total, grad_rows, row_delta, head_scale):
    scores = jnp.dot(query_rows, key_rows.T, preferred_element_type=jnp.float32) * head_scale
    prob_rows = jnp.where(allowed, jnp.exp(scores - log_total[:, None]), 0.0)
    prob_bf = prob_rows.astype(jnp.bfloat16)
    value_gradient_rows = jnp.dot(prob_bf.T, grad_rows, preferred_element_type=jnp.float32)
    prob_grad = jnp.dot(grad_rows, value_rows.T, preferred_element_type=jnp.float32)
    score_grad = (prob_rows * (prob_grad - row_delta[:, None]) * head_scale).astype(jnp.bfloat16)
    query_grad = jnp.dot(score_grad, key_rows, preferred_element_type=jnp.float32)
    key_gradient_rows = jnp.dot(score_grad.T, query_rows, preferred_element_type=jnp.float32)
    return (query_grad, key_gradient_rows, value_gradient_rows)

def reference(tokens, cotangent, block_order, attn_gain, w_query, key_weight, value_weight, w_out, query_gain, key_gain, mlp_gain, w_gate, w_up, w_down):
    row_ids = jnp.arange(SEQUENCE_TOKENS, dtype=jnp.int32)
    token_pos = (block_order[(row_ids // BLKLEN).astype(jnp.int32)] * BLKLEN + row_ids % BLKLEN).astype(jnp.int32)
    allowed = token_pos[None, :] <= token_pos[:, None]
    cosine, sine_table = rope_tables(token_pos)
    head_scale = HEAD_SIZE ** (-0.5)
    query_group_size = QUERY_HEADS // KEY_VALUE_HEADS
    attn_gain_f = attn_gain.astype(jnp.float32)
    mlp_gain_f = mlp_gain.astype(jnp.float32)
    query_gain_f = query_gain.astype(jnp.float32)
    key_gain_float = key_gain.astype(jnp.float32)

    def one_sequence(totals, inputs):
        tokens_row, cotangent_row = inputs
        tokens_f = tokens_row.astype(jnp.float32)
        normed_in, inverse_in = normalize(tokens_f)
        attention_input = (normed_in * attn_gain_f).astype(jnp.bfloat16)
        query = matrix_product(attention_input, w_query).reshape(SEQUENCE_TOKENS, QUERY_HEADS, HEAD_SIZE)
        key_projected = matrix_product(attention_input, key_weight).reshape(SEQUENCE_TOKENS, KEY_VALUE_HEADS, HEAD_SIZE)
        value_states = matrix_product(attention_input, value_weight).astype(jnp.bfloat16).reshape(SEQUENCE_TOKENS, KEY_VALUE_HEADS, HEAD_SIZE)
        query_hat, query_inv = normalize(query)
        key_normalized, key_inverse_norm = normalize(key_projected)
        rot_query = rotate(query_hat * query_gain_f, cosine, sine_table).astype(jnp.bfloat16)
        rot_key = rotate(key_normalized * key_gain_float, cosine, sine_table).astype(jnp.bfloat16)
        head_queries = jnp.transpose(rot_query, (1, 0, 2))
        head_keys = jnp.repeat(jnp.transpose(rot_key, (1, 0, 2)), query_group_size, axis=0)
        head_values = jnp.repeat(jnp.transpose(value_states, (1, 0, 2)), query_group_size, axis=0)

        def forward_head(head_items):
            return attention_head(head_items[0], head_items[1], head_items[2], allowed, head_scale)
        head_out, head_lse = lax.map(forward_head, (head_queries, head_keys, head_values))
        attn_heads = jnp.transpose(head_out, (1, 0, 2)).reshape(SEQUENCE_TOKENS, QUERY_HEADS * HEAD_SIZE)
        attn_heads_bf = attn_heads.astype(jnp.bfloat16)
        resid = tokens_f + matrix_product(attn_heads_bf, w_out)
        normed_mid, inverse_mid = normalize(resid)
        mlp_input = (normed_mid * mlp_gain_f).astype(jnp.bfloat16)
        gate_proj = matrix_product(mlp_input, w_gate)
        up_proj = matrix_product(mlp_input, w_up)
        gate_sigmoid = jax.nn.sigmoid(gate_proj)
        gate_silu = gate_proj * gate_sigmoid
        activation = (gate_silu * up_proj).astype(jnp.bfloat16)
        layer_out = (resid + matrix_product(activation, w_down)).astype(jnp.bfloat16)
        grad_down = matrix_product(activation.T, cotangent_row)
        grad_act = matrix_product(cotangent_row, w_down.T)
        grad_up_bf = (grad_act * gate_silu).astype(jnp.bfloat16)
        grad_gate_bf = (grad_act * up_proj * gate_sigmoid * (1.0 + gate_proj * (1.0 - gate_sigmoid))).astype(jnp.bfloat16)
        grad_gate_w = matrix_product(mlp_input.T, grad_gate_bf)
        grad_up_w = matrix_product(mlp_input.T, grad_up_bf)
        grad_mid = matrix_product(grad_gate_bf, w_gate.T) + matrix_product(grad_up_bf, w_up.T)
        grad_mlp_gain = lax.optimization_barrier(jnp.sum(grad_mid * normed_mid, axis=0))
        grad_resid = cotangent_row.astype(jnp.float32) + normalize_backward(grad_mid, normed_mid, inverse_mid, mlp_gain_f)
        grad_resid_bf = grad_resid.astype(jnp.bfloat16)
        grad_out_w = matrix_product(attn_heads_bf.T, grad_resid_bf)
        grad_heads = matrix_product(grad_resid_bf, w_out.T).reshape(SEQUENCE_TOKENS, QUERY_HEADS, HEAD_SIZE)
        row_delta = jnp.transpose(lax.optimization_barrier(jnp.sum(grad_heads * attn_heads.reshape(SEQUENCE_TOKENS, QUERY_HEADS, HEAD_SIZE), axis=-1)), (1, 0))
        grad_heads_bf = jnp.transpose(grad_heads.astype(jnp.bfloat16), (1, 0, 2))

        def backward_head(head_items):
            return attention_head_back(head_items[0], head_items[1], head_items[2], allowed, head_items[3], head_items[4], head_items[5], head_scale)
        query_grad, key_gradient_rows, value_gradient_rows = lax.map(backward_head, (head_queries, head_keys, head_values, head_lse, grad_heads_bf, row_delta))
        grad_rot_query = jnp.transpose(query_grad, (1, 0, 2))
        rotated_key_gradient = jnp.transpose(lax.optimization_barrier(jnp.sum(key_gradient_rows.reshape(KEY_VALUE_HEADS, query_group_size, SEQUENCE_TOKENS, HEAD_SIZE), axis=1)), (1, 0, 2))
        value_gradient = jnp.transpose(lax.optimization_barrier(jnp.sum(value_gradient_rows.reshape(KEY_VALUE_HEADS, query_group_size, SEQUENCE_TOKENS, HEAD_SIZE), axis=1)), (1, 0, 2))
        grad_query_n = rotate_back(grad_rot_query, cosine, sine_table)
        key_gradient_normed = rotate_back(rotated_key_gradient, cosine, sine_table)
        grad_query_gain = lax.optimization_barrier(jnp.sum(grad_query_n * query_hat, axis=(0, 1)))
        grad_key_gain = lax.optimization_barrier(jnp.sum(key_gradient_normed * key_normalized, axis=(0, 1)))
        grad_query_bf = normalize_backward(grad_query_n, query_hat, query_inv, query_gain_f).astype(jnp.bfloat16).reshape(SEQUENCE_TOKENS, QUERY_HEADS * HEAD_SIZE)
        key_gradient_half = normalize_backward(key_gradient_normed, key_normalized, key_inverse_norm, key_gain_float).astype(jnp.bfloat16).reshape(SEQUENCE_TOKENS, KEY_VALUE_HEADS * HEAD_SIZE)
        value_gradient_half = value_gradient.astype(jnp.bfloat16).reshape(SEQUENCE_TOKENS, KEY_VALUE_HEADS * HEAD_SIZE)
        grad_query_w = matrix_product(attention_input.T, grad_query_bf)
        grad_key_w = matrix_product(attention_input.T, key_gradient_half)
        grad_value_w = matrix_product(attention_input.T, value_gradient_half)
        grad_in = matrix_product(grad_query_bf, w_query.T) + matrix_product(key_gradient_half, key_weight.T) + matrix_product(value_gradient_half, value_weight.T)
        grad_attn_gain = lax.optimization_barrier(jnp.sum(grad_in * normed_in, axis=0))
        tokens_grad = grad_resid + normalize_backward(grad_in, normed_in, inverse_in, attn_gain_f)
        new_terms = (grad_attn_gain, grad_query_w, grad_key_w, grad_value_w, grad_out_w, grad_query_gain, grad_key_gain, grad_mlp_gain, grad_gate_w, grad_up_w, grad_down)
        totals = tuple((total_now + term_now for total_now, term_now in zip(totals, new_terms)))
        return (totals, (layer_out, tokens_grad))
    params = (attn_gain, w_query, key_weight, value_weight, w_out, query_gain, key_gain, mlp_gain, w_gate, w_up, w_down)
    start_totals = tuple((jnp.zeros(param.shape, jnp.float32) for param in params))
    totals, (layer_out, tokens_grad) = lax.scan(one_sequence, start_totals, (tokens, cotangent))
    return (layer_out, tokens_grad, totals[0], totals[1], totals[2], totals[3], totals[4], totals[5], totals[6], totals[7], totals[8], totals[9], totals[10])
```

```python
import functools

import jax
import jax.numpy as jnp
from jax import lax
from jax.experimental import pallas as pl
from jax.experimental.pallas import tpu as pltpu
from jax.sharding import PartitionSpec as P


HEAD_SIZE = 128
BLKLEN = 128
LANES = 128

EPSILON = 1e-06
THETA = 1000000.0
NEG_LARGE = -1e30

BF = jnp.bfloat16
F32 = jnp.float32


def shifted(value, axis, by):
    count = lax.axis_size(axis)
    return lax.ppermute(value, axis, [(i, (i + by) % count) for i in range(count)])


def swapped(value, axis):
    count = lax.axis_size(axis)
    return lax.ppermute(value, axis, [(i, i ^ 1) for i in range(count)])


def in_order(pieces, first, step):
    if len(pieces) <= 2:
        return functools.reduce(jnp.add, pieces)
    count = len(pieces)
    stacked = jnp.stack(pieces if step == 1 else [pieces[0]] + pieces[:0:-1])
    stacked = lax.dynamic_slice_in_dim(
        jnp.concatenate([stacked, stacked]), (count - first) % count, count
    )
    return functools.reduce(jnp.add, [stacked[i] for i in range(count)])


def small_sum(value, axis):
    count = lax.axis_size(axis)
    if count & (count - 1):
        return lax.psum(value, axis)
    by = 1
    while by < count:
        value = value + lax.ppermute(value, axis, [(i, i ^ by) for i in range(count)])
        by *= 2
    return value


def nn(left, right):
    return lax.dot_general(left, right, (((1,), (0,)), ((), ())), preferred_element_type=F32)


def nt(left, right):
    return lax.dot_general(left, right, (((1,), (1,)), ((), ())), preferred_element_type=F32)


def tn(left, right):
    return lax.dot_general(left, right, (((0,), (0,)), ((), ())), preferred_element_type=F32)


def struct(shape, dtype):
    return jax.ShapeDtypeStruct(shape, dtype)


def kernel(body, outs, ids, *operands, scratch=()):
    specs = [pl.BlockSpec(memory_space=pltpu.SMEM)]
    specs += [pl.BlockSpec(memory_space=pltpu.VMEM) for _ in operands]
    return pl.pallas_call(
        body,
        out_shape=outs,
        in_specs=specs,
        out_specs=[pl.BlockSpec(memory_space=pltpu.VMEM) for _ in outs],
        scratch_shapes=list(scratch),
    )(ids, *operands)


def inverse_norm(values):
    return lax.rsqrt(jnp.mean(values * values, axis=-1, keepdims=True) + EPSILON)


def back_norm(grad_in, normed, inverse, gain_row):
    scaled = grad_in * gain_row
    return inverse * (scaled - normed * jnp.mean(scaled * normed, axis=-1, keepdims=True))


def half_roll(values):
    return pltpu.roll(values, HEAD_SIZE // 2, 1)


def head(h):
    return slice(h * HEAD_SIZE, (h + 1) * HEAD_SIZE)


def aligned(start, by):
    return pl.multiple_of(start, by)


class Sizes:
    pass


def rows_of(ids_ref, first, rows, shape, dim):
    index = lax.broadcasted_iota(jnp.int32, shape, dim)
    pos = jnp.zeros(shape, jnp.int32)
    for b in range(rows // BLKLEN):
        here = ids_ref[first + b] * BLKLEN + (index - b * BLKLEN)
        pos = jnp.where(index >= b * BLKLEN, here, pos)
    return pos


TP_ID = 0
BLOCK_IDS = 1


def project(z, ids, tokens, gain, cosine, sine, qgain, kgain, pieces):
    rows, width = tokens.shape
    qw, kw = z.qw, z.kw

    def body(ids_ref, tok, gain_r, cos_r, sin_r, qg, kg, *refs):
        ws = refs[: len(pieces)]
        h1_r, q_r, k_r, qr_r, kv_r = refs[len(pieces) :]
        x = tok[...].astype(F32)
        h1 = (x * inverse_norm(x) * gain_r[...]).astype(BF)
        h1_r[...] = h1
        at, acc = 0, None
        for w in ws:
            n = w.shape[0]
            part = nn(h1[:, at : at + n], w[...])
            acc = part if acc is None else acc + part
            at += n
        q_r[...] = acc[:, :qw]
        k_r[...] = acc[:, qw : qw + kw]
        kv_r[:, kw:] = acc[:, qw + kw :].astype(BF)
        cos, sin = cos_r[...], sin_r[...]
        for h in range(qw // HEAD_SIZE):
            a = acc[:, head(h)]
            a = a * inverse_norm(a) * qg[...]
            qr_r[:, head(h)] = (a * cos + half_roll(a) * sin).astype(BF)
        for h in range(kw // HEAD_SIZE):
            a = acc[:, qw + h * HEAD_SIZE : qw + (h + 1) * HEAD_SIZE]
            a = a * inverse_norm(a) * kg[...]
            kv_r[:, head(h)] = (a * cos + half_roll(a) * sin).astype(BF)

    outs = [
        struct((rows, width), BF),
        struct((rows, qw), F32),
        struct((rows, kw), F32),
        struct((rows, qw), BF),
        struct((rows, 2 * kw), BF),
    ]
    return kernel(body, outs, ids, tokens, gain, cosine, sine, qgain, kgain, *pieces)


def attend(z, ids, queries, kvs, wout):
    rows, qw = queries.shape
    kw, group, scale = z.kw, z.group, HEAD_SIZE**-0.5
    width, chunk, tps = z.width, rows // z.tp, z.tp
    nkv, nw = len(kvs), len(wout)

    def body(ids_ref, q_ref, *refs):
        kv_refs, w_refs = refs[:nkv], refs[nkv : nkv + nw]
        o_r, ob_r, lse_r = refs[nkv + nw : nkv + nw + 3]
        outs = refs[nkv + nw + 3 : nkv + nw + 3 + tps]
        part_r = refs[-1]
        lane = lax.broadcasted_iota(jnp.int32, (BLKLEN, LANES), 1)
        for r in range(rows // BLKLEN):
            span = slice(r * BLKLEN, (r + 1) * BLKLEN)
            row_pos = ids_ref[BLOCK_IDS + r] * BLKLEN + lax.broadcasted_iota(
                jnp.int32, (BLKLEN, rows), 0
            )
            masks = [
                rows_of(ids_ref, BLOCK_IDS + b * (rows // BLKLEN), rows, (BLKLEN, rows), 1)
                <= row_pos
                for b in range(nkv)
            ]
            logs = jnp.zeros((BLKLEN, LANES), F32)
            for h in range(qw // HEAD_SIZE):
                g = h // group
                q = q_ref[span, head(h)]
                scores = [
                    jnp.where(masks[b], nt(q, kv_refs[b][:, head(g)]) * scale, NEG_LARGE)
                    for b in range(nkv)
                ]
                best = functools.reduce(jnp.maximum, scores)
                best = jnp.max(best, axis=-1, keepdims=True)
                total, out = None, None
                for b in range(nkv):
                    w = jnp.exp(scores[b] - best)
                    part = nn(w.astype(BF), kv_refs[b][:, kw + g * HEAD_SIZE : kw + (g + 1) * HEAD_SIZE])
                    total = w if total is None else total + w
                    out = part if out is None else out + part
                total = jnp.sum(total, axis=-1, keepdims=True)
                out = out / total
                o_r[span, head(h)] = out
                ob_r[span, head(h)] = out.astype(BF)
                logs = jnp.where(lane == h, best + jnp.log(total), logs)
            lse_r[span, :] = logs
        ob = ob_r[...]
        at = 0
        for w in w_refs:
            n = w.shape[1]
            part_r[:, at : at + n] = nn(ob, w[...])
            at += n
        t = ids_ref[TP_ID]
        for k in range(tps):
            start = aligned(lax.rem(t + k, tps) * chunk, chunk)
            outs[k][...] = part_r[pl.ds(start, chunk), :].astype(outs[k].dtype)

    outs = [struct((rows, qw), F32), struct((rows, qw), BF), struct((rows, LANES), F32)]
    outs += [struct((chunk, width), F32 if k == 0 else BF) for k in range(tps)]
    got = kernel(
        body, outs, ids, queries, *kvs, *wout, scratch=[pltpu.VMEM((rows, width), F32)]
    )
    return got[0], got[1], got[2], list(got[3:])


def middle(z, ids, parts, tokens, gain):
    chunk, width = parts[0].shape

    def body(ids_ref, *refs):
        ps = refs[: len(parts)]
        tok, gain_r, r2_r, h2_r = refs[len(parts) :]
        start = aligned(ids_ref[TP_ID] * chunk, chunk)
        r2 = tok[pl.ds(start, chunk), :].astype(F32)
        r2 = r2 + functools.reduce(jnp.add, [p[...].astype(F32) for p in ps])
        r2_r[...] = r2
        h2_r[...] = (r2 * inverse_norm(r2) * gain_r[...]).astype(BF)

    outs = [struct((chunk, width), F32), struct((chunk, width), BF)]
    return kernel(body, outs, ids, *parts, tokens, gain)


def gathered_rows(z, ids_ref, refs, full_ref):
    chunk = refs[0].shape[0]
    for k, ref in enumerate(refs):
        owner = lax.rem(ids_ref[TP_ID] + z.tp - k, z.tp)
        full_ref[pl.ds(aligned(owner * chunk, chunk), chunk), :] = ref[...]


def feed_forward(z, ids, h2_parts, dact, wgu):
    chunk, width = h2_parts[0].shape
    tps, ff, rows = z.tp, z.ff, chunk * z.tp
    nh, nw = len(h2_parts), len(wgu)
    step = 256 if ff % 256 == 0 else ff

    def body(ids_ref, *refs):
        parts, dact_r, ws = refs[:nh], refs[nh], refs[nh + 1 : nh + 1 + nw]
        h2_r, act_r, dgu_r = refs[nh + 1 + nw : nh + 4 + nw]
        outs = refs[nh + 4 + nw : nh + 4 + nw + tps]
        sum_r = refs[-1]
        gathered_rows(z, ids_ref, parts, h2_r)
        for j in range(0, ff, step):
            gate, up = None, None
            at = 0
            for w in ws:
                n = w.shape[0]
                h = h2_r[:, at : at + n]
                g = nn(h, w[:, j : j + step])
                u = nn(h, w[:, ff + j : ff + j + step])
                gate = g if gate is None else gate + g
                up = u if up is None else up + u
                at += n
            sig = jax.nn.sigmoid(gate)
            silu = gate * sig
            d = dact_r[:, j : j + step]
            act_r[:, j : j + step] = (silu * up).astype(BF)
            dgu_r[:, ff + j : ff + j + step] = (d * silu).astype(BF)
            dgu_r[:, j : j + step] = (d * up * sig * (1.0 + gate * (1.0 - sig))).astype(BF)
        at = 0
        for w in ws:
            n = w.shape[0]
            sum_r[:, at : at + n] = nt(dgu_r[...], w[...])
            at += n
        t = ids_ref[TP_ID]
        for k in range(tps):
            start = aligned(lax.rem(t + k, tps) * chunk, chunk)
            outs[k][...] = sum_r[pl.ds(start, chunk), :].astype(outs[k].dtype)

    outs = [struct((rows, width), BF), struct((rows, ff), BF), struct((rows, 2 * ff), BF)]
    outs += [struct((chunk, width), F32 if k == 0 else BF) for k in range(tps)]
    got = kernel(
        body, outs, ids, *h2_parts, dact, *wgu, scratch=[pltpu.VMEM((rows, width), F32)]
    )
    return got[0], got[1], got[2], list(got[3:])


def down(z, ids, act, wd):
    rows, tps, width = act.shape[0], z.tp, z.width
    chunk = rows // tps

    def body(ids_ref, act_r, *refs):
        ws, outs, part_r = refs[: len(wd)], refs[len(wd) : -1], refs[-1]
        at = 0
        for w in ws:
            n = w.shape[1]
            part_r[:, at : at + n] = nn(act_r[...], w[...])
            at += n
        t = ids_ref[TP_ID]
        for k in range(tps):
            start = aligned(lax.rem(t + k, tps) * chunk, chunk)
            outs[k][...] = part_r[pl.ds(start, chunk), :].astype(outs[k].dtype)

    outs = [struct((chunk, width), F32 if k == 0 else BF) for k in range(tps)]
    return list(kernel(body, outs, ids, act, *wd, scratch=[pltpu.VMEM((rows, width), F32)]))


def middle_back(z, ids, parts, r2, cot, gain):
    chunk, width = r2.shape

    def body(ids_ref, *refs):
        ps = refs[: len(parts)]
        r2_r, cot_r, gain_r, d_r, db_r, g_r = refs[len(parts) :]
        grad = functools.reduce(jnp.add, [p[...].astype(F32) for p in ps])
        r = r2_r[...]
        inv = inverse_norm(r)
        xhat = r * inv
        g_r[...] = jnp.sum(grad * xhat, axis=0, keepdims=True)
        start = aligned(ids_ref[TP_ID] * chunk, chunk)
        d = cot_r[pl.ds(start, chunk), :].astype(F32) + back_norm(grad, xhat, inv, gain_r[...])
        d_r[...] = d
        db_r[...] = d.astype(BF)

    outs = [struct((chunk, width), F32), struct((chunk, width), BF), struct((1, width), F32)]
    return kernel(body, outs, ids, *parts, r2, cot, gain)


def attend_back(z, ids, d_parts, wout, out, lse, queries, kvs):
    chunk, width = d_parts[0].shape
    rows, qw = queries.shape
    kw, group, scale = z.kw, z.group, HEAD_SIZE**-0.5
    nd, nw, nkv = len(d_parts), len(wout), len(kvs)

    def body(ids_ref, *refs):
        parts, ws = refs[:nd], refs[nd : nd + nw]
        o_r, lse_r, q_ref = refs[nd + nw : nd + nw + 3]
        kv_refs = refs[nd + nw + 3 : nd + nw + 3 + nkv]
        db_r, dq_r = refs[nd + nw + 3 + nkv : nd + nw + 5 + nkv]
        dkv_r = refs[nd + nw + 5 + nkv :]
        gathered_rows(z, ids_ref, parts, db_r)
        at, do = 0, None
        for w in ws:
            n = w.shape[1]
            part = nt(db_r[:, at : at + n], w[...])
            do = part if do is None else do + part
            at += n
        logs = lse_r[...].T
        row_pos = rows_of(ids_ref, BLOCK_IDS, rows, (rows, rows), 1)
        masks = [
            rows_of(ids_ref, BLOCK_IDS + b * (rows // BLKLEN), rows, (rows, rows), 0) <= row_pos
            for b in range(nkv)
        ]
        lane = lax.broadcasted_iota(jnp.int32, (rows, LANES), 1)
        deltas = jnp.zeros((rows, LANES), F32)
        for h in range(qw // HEAD_SIZE):
            delta = jnp.sum(do[:, head(h)] * o_r[:, head(h)], axis=-1, keepdims=True)
            deltas = jnp.where(lane == h, delta, deltas)
        deltas = deltas.T
        for g in range(kw // HEAD_SIZE):
            vs = slice(kw + g * HEAD_SIZE, kw + (g + 1) * HEAD_SIZE)
            dks, dvs = [None] * nkv, [None] * nkv
            for h in range(g * group, (g + 1) * group):
                q = q_ref[:, head(h)]
                dob = do[:, head(h)].astype(BF)
                log_row, delta_row = logs[h : h + 1, :], deltas[h : h + 1, :]
                dq = None
                for b in range(nkv):
                    k, v = kv_refs[b][:, head(g)], kv_refs[b][:, vs]
                    s = nt(k, q) * scale
                    p = jnp.exp(jnp.where(masks[b], s, NEG_LARGE) - log_row)
                    dv = nn(p.astype(BF), dob)
                    ds = (p * (nt(v, dob) - delta_row) * scale).astype(BF)
                    dk = nn(ds, q)
                    part = tn(ds, k)
                    dq = part if dq is None else dq + part
                    dks[b] = dk if dks[b] is None else dks[b] + dk
                    dvs[b] = dv if dvs[b] is None else dvs[b] + dv
                dq_r[:, head(h)] = dq
            for b in range(nkv):
                dkv_r[b][:, head(g)] = dks[b].astype(dkv_r[b].dtype)
                dkv_r[b][:, vs] = dvs[b].astype(dkv_r[b].dtype)

    outs = [struct((rows, width), BF), struct((rows, qw), F32)]
    outs += [struct((rows, 2 * kw), F32 if z.kept(b) else BF) for b in range(nkv)]
    got = kernel(body, outs, ids, *d_parts, *wout, out, lse, queries, *kvs)
    return got[0], got[1], list(got[2:])


def unrope(grad, raw, cos, sin, gain):
    grad = grad * cos - half_roll(grad) * sin
    inv = inverse_norm(raw)
    normed = raw * inv
    gain_part = jnp.sum(grad * normed, axis=0, keepdims=True)
    return back_norm(grad, normed, inv, gain).astype(BF), gain_part


def query_back(z, ids, dq, q, cosine, sine, qgain, pieces):
    rows, qw = q.shape

    def body(ids_ref, dq_r, q_r, cos_r, sin_r, qg, *refs):
        ws = refs[: len(pieces)]
        dqb_r, dh_r, g_r = refs[len(pieces) :]
        total = None
        for h in range(qw // HEAD_SIZE):
            grad, part = unrope(dq_r[:, head(h)], q_r[:, head(h)], cos_r[...], sin_r[...], qg[...])
            dqb_r[:, head(h)] = grad
            total = part if total is None else total + part
        g_r[...] = total
        at = 0
        for w in ws:
            n = w.shape[0]
            dh_r[:, at : at + n] = nt(dqb_r[...], w[:, :qw])
            at += n

    outs = [struct((rows, qw), BF), struct((rows, z.width), F32), struct((1, HEAD_SIZE), F32)]
    return kernel(body, outs, ids, dq, q, cosine, sine, qgain, *pieces)


def key_back(z, ids, dkvs, k, cosine, sine, kgain, dh, tokens, pieces):
    rows, kw = k.shape
    qw, tps, width = z.qw, z.tp, z.width
    chunk = rows // tps
    nd, nw = len(dkvs), len(pieces)

    def body(ids_ref, *refs):
        ds, (k_r, cos_r, sin_r, kg, dh_r, tok) = refs[:nd], refs[nd : nd + 6]
        ws = refs[nd + 6 : nd + 6 + nw]
        dkvb_r, kg_r, ag_r = refs[nd + 6 + nw : nd + 9 + nw]
        outs, sum_r = refs[nd + 9 + nw : -1], refs[-1]
        total = None
        for h in range(kw // HEAD_SIZE):
            grad = functools.reduce(jnp.add, [d[:, head(h)].astype(F32) for d in ds])
            grad, part = unrope(grad, k_r[:, head(h)], cos_r[...], sin_r[...], kg[...])
            dkvb_r[:, head(h)] = grad
            total = part if total is None else total + part
        kg_r[...] = total
        grad = functools.reduce(jnp.add, [d[:, kw:].astype(F32) for d in ds])
        dkvb_r[:, kw:] = grad.astype(BF)
        at = 0
        for w in ws:
            n = w.shape[0]
            sum_r[:, at : at + n] = dh_r[:, at : at + n] + nt(dkvb_r[...], w[:, qw:])
            at += n
        t = ids_ref[TP_ID]
        for j in range(tps):
            start = aligned(lax.rem(t + j, tps) * chunk, chunk)
            outs[j][...] = sum_r[pl.ds(start, chunk), :].astype(outs[j].dtype)
        x = tok[...].astype(F32)
        ag_r[...] = jnp.sum(sum_r[...] * (x * inverse_norm(x)), axis=0, keepdims=True)

    outs = [struct((rows, 2 * kw), BF), struct((1, HEAD_SIZE), F32), struct((1, width), F32)]
    outs += [struct((chunk, width), F32 if j == 0 else BF) for j in range(tps)]
    got = kernel(
        body,
        outs,
        ids,
        *dkvs,
        k,
        cosine,
        sine,
        kgain,
        dh,
        tokens,
        *pieces,
        scratch=[pltpu.VMEM((rows, width), F32)],
    )
    return got[0], got[1], got[2], list(got[3:])


def last(z, ids, parts, tokens, gain, d_mid):
    chunk, width = d_mid.shape

    def body(ids_ref, *refs):
        ps = refs[: len(parts)]
        tok, gain_r, d_r, out_r = refs[len(parts) :]
        grad = functools.reduce(jnp.add, [p[...].astype(F32) for p in ps])
        start = aligned(ids_ref[TP_ID] * chunk, chunk)
        x = tok[pl.ds(start, chunk), :].astype(F32)
        inv = inverse_norm(x)
        out_r[...] = (d_r[...] + back_norm(grad, x * inv, inv, gain_r[...])).astype(BF)

    return kernel(body, [struct((chunk, width), BF)], ids, *parts, tokens, gain, d_mid)[0]


def per_device(
    tokens,
    cotangent,
    block_order,
    attn_gain,
    w_query,
    key_weight,
    value_weight,
    w_out,
    query_gain,
    key_gain,
    mlp_gain,
    w_gate,
    w_up,
    w_down,
):
    shards, ctxs, tps = (lax.axis_size(a) for a in ("shard", "ctx", "tp"))
    shard, ctx, tp = (lax.axis_index(a) for a in ("shard", "ctx", "tp"))
    own, rows, width = attn_gain.shape[0], tokens.shape[1], tokens.shape[2]
    pair = 2 if ctxs % 2 == 0 else 1
    share = pair if own % (2 * LANES) == 0 else 1
    half = lax.rem(ctx, 2) if share == 2 else jnp.int32(0)
    part = own // share
    z = Sizes()
    z.qw, z.kw, z.ff = w_query.shape[1], key_weight.shape[1], w_gate.shape[1]
    z.group, z.tp, z.width = z.qw // z.kw, tps, width
    z.kept = lambda b: b % pair == 0

    def turned(value, count, at):
        size = value.shape[-1] // count
        both = jnp.concatenate([value, value], axis=-1)
        return lax.dynamic_slice_in_dim(both, at * size, value.shape[-1], axis=both.ndim - 1)

    def halves(block):
        if share == 1:
            return block
        a, b = block[..., :part], block[..., part:]
        return jnp.where(half == 0, block, jnp.concatenate([b, a], axis=-1))

    def to_held(value):
        value = turned(value, shards, shard)
        blocks = [value[..., i * own : (i + 1) * own] for i in range(shards)]
        return jnp.concatenate([blocks[0]] + [halves(b) for b in blocks[1:]], axis=-1)

    def from_held(value):
        blocks = [value[..., i * own : (i + 1) * own] for i in range(shards)]
        value = jnp.concatenate([blocks[0]] + [halves(b) for b in blocks[1:]], axis=-1)
        return turned(value, shards, lax.rem(shards - shard, shards))

    def gather(value, dim):
        send = value
        if share == 2:
            send = lax.dynamic_slice_in_dim(value, half * part, part, axis=dim)
        pieces = []
        for k in range(1, shards):
            got = shifted(send, "shard", -k)
            pieces.append(got)
            if share == 2:
                pieces.append(swapped(got, "ctx"))
        return pieces

    def whole(value, pieces, dim):
        pieces = [value] + pieces
        if own % LANES:
            return [jnp.concatenate(pieces, axis=dim)]
        return pieces

    packed = jnp.concatenate([attn_gain, mlp_gain, query_gain, key_gain])
    gain_rows = [packed] + [shifted(packed, "shard", -k) for k in range(1, shards)]
    wqkv = jnp.concatenate([w_query, key_weight, value_weight], axis=1)
    wqkv = whole(wqkv, gather(wqkv, 0), 0)
    wout = whole(w_out, gather(w_out, 1), 1)
    wgu = jnp.concatenate([w_gate, w_up], axis=1)
    wgu = whole(wgu, gather(wgu, 0), 0)
    wdown = whole(w_down, gather(w_down, 1), 1)

    qk = query_gain.shape[0]
    spans = [(0, own), (own, 2 * own), (2 * own, 2 * own + qk), (2 * own + qk, 2 * own + 2 * qk)]
    gains = [
        turned(
            jnp.concatenate([r[a:b] for r in gain_rows])[None], shards, lax.rem(shards - shard, shards)
        ).astype(F32)
        for a, b in spans
    ]
    gain1, gain2, qgain, kgain = to_held(gains[0]), to_held(gains[1]), gains[2], gains[3]

    owners = [ctx]
    if pair == 2:
        owners.append(ctx ^ 1)
    for j in range(1, ctxs // pair):
        owners.append(lax.rem(ctx + ctxs - j * pair, ctxs))
        if pair == 2:
            owners.append(lax.rem((ctx ^ 1) + ctxs - j * pair, ctxs))
    blocks = rows // BLKLEN
    order = block_order.reshape(ctxs, blocks)
    ids = jnp.concatenate(
        [tp[None]] + [lax.dynamic_slice_in_dim(order, o, 1, axis=0)[0] for o in owners]
    ).astype(jnp.int32)

    half_width = HEAD_SIZE // 2
    frequency = 1.0 / THETA ** (jnp.arange(half_width, dtype=F32) * 2.0 / HEAD_SIZE)
    local = (ids[1 : 1 + blocks, None] * BLKLEN + jnp.arange(BLKLEN, dtype=jnp.int32)).reshape(rows)
    angles = local.astype(F32)[:, None] * frequency[None, :]
    cos_half, sin_half = jnp.cos(angles), jnp.sin(angles)
    cosine = jnp.concatenate([cos_half, cos_half], axis=1)
    sine = jnp.concatenate([-sin_half, sin_half], axis=1)

    tok = to_held(tokens[0])
    cot = to_held(cotangent[0])

    def scatter_rows(chunks):
        return [chunks[0]] + [shifted(chunks[k], "tp", k) for k in range(1, tps)]

    def gather_rows(chunk):
        return [chunk] + [shifted(chunk, "tp", k) for k in range(1, tps)]

    def full_rows(chunks):
        stacked = jnp.concatenate(chunks[:1] + chunks[:0:-1])
        both = jnp.concatenate([stacked, stacked])
        size = chunks[0].shape[0]
        return lax.dynamic_slice_in_dim(both, lax.rem(tps - tp, tps) * size, rows, axis=0)

    h1, q, k, qr, kv = project(z, ids, tok, gain1, cosine, sine, qgain, kgain, wqkv)
    kvs = [kv]
    far = [shifted(kv, "ctx", j * pair) for j in range(1, ctxs // pair)]
    if pair == 2:
        kvs.append(swapped(kv, "ctx"))
    for got in far:
        kvs.append(got)
        if pair == 2:
            kvs.append(swapped(got, "ctx"))
    out, out_bf, lse, chunks = attend(z, ids, qr, kvs, wout)
    r2, h2_chunk = middle(z, ids, scatter_rows(chunks), tok, gain2)
    h2_parts = gather_rows(h2_chunk)
    at, dact = 0, None
    for w in wdown:
        n = w.shape[1]
        term = nt(cot[:, at : at + n], w)
        dact = term if dact is None else dact + term
        at += n
    h2, act, dgu, chunks = feed_forward(z, ids, h2_parts, dact, wgu)
    mid_parts = scatter_rows(chunks)

    def reduced(left, right):
        columns = right.shape[1]
        total = tn(left, right)
        mine = total[:own]
        others = [total[i * own : (i + 1) * own] for i in range(1, shards)]
        if share == 2:
            keep = lax.dynamic_slice_in_dim(mine, half * part, part)
            give = lax.dynamic_slice_in_dim(mine, (1 - half) * part, part)
            give = jnp.concatenate([give] + [o[part:] for o in others]).astype(BF)
            got = swapped(give, "ctx").astype(F32)
            mine = keep + got[:part]
            others = [
                o[:part] + got[(i + 1) * part : (i + 2) * part] for i, o in enumerate(others)
            ]
        for i, o in enumerate(others):
            mine = mine + shifted(o.astype(BF), "shard", i + 1).astype(F32)
        mine = mine.astype(BF)
        steps = ctxs // share
        parts = [mine] + [shifted(mine, "ctx", j * share) for j in range(1, steps)]
        mine = in_order([p.astype(F32) for p in parts], ctx // share, -1)
        if share == 2:
            other = swapped(mine, "ctx")
            mine = jnp.where(
                half == 0, jnp.concatenate([mine, other]), jnp.concatenate([other, mine])
            )
        return mine

    down_parts = scatter_rows(down(z, ids, act, wdown))
    gu_g = reduced(h2, dgu)
    down_g = reduced(cot, act)

    dr2, dr2_chunk, mlp_part = middle_back(z, ids, mid_parts, r2, cot, gain2)
    dr2b, dq, dkvs = attend_back(
        z, ids, gather_rows(dr2_chunk), wout, out, lse, qr, kvs
    )
    start = aligned_rows = None
    out_chunk = (r2 + functools.reduce(jnp.add, [p.astype(F32) for p in down_parts])).astype(BF)
    layer_out = from_held(full_rows(gather_rows(out_chunk)))

    if pair == 2:
        got = swapped(jnp.concatenate([dkvs[b] for b in range(1, len(dkvs), 2)]), "ctx")
        sums = [
            (dkvs[2 * i], got[i * rows : (i + 1) * rows]) for i in range(len(dkvs) // 2)
        ]
    else:
        sums = [(d,) for d in dkvs]
    own_terms = list(sums[0])
    for j in range(1, len(sums)):
        total = functools.reduce(jnp.add, [t.astype(F32) for t in sums[j]])
        own_terms.append(shifted(total.astype(BF), "ctx", -j * pair))

    dqb, dh, q_part = query_back(z, ids, dq, q, cosine, sine, qgain, wqkv)
    out_g = reduced(dr2b, out_bf)
    query_g = reduced(h1, dqb)
    dkvb, k_part, attn_part, chunks = key_back(
        z, ids, own_terms, k, cosine, sine, kgain, dh, tok, wqkv
    )
    in_parts = scatter_rows(chunks)
    kv_g = reduced(h1, dkvb)
    small = jnp.concatenate([from_held(attn_part), from_held(mlp_part), q_part, k_part], axis=1)
    small = small_sum(small_sum(small_sum(small, "tp"), "ctx"), "shard")[0]
    in_chunk = last(z, ids, in_parts, tok, gain1, dr2)
    tokens_grad = from_held(full_rows(gather_rows(in_chunk))).astype(F32)

    def mine_of(value, size):
        return lax.dynamic_slice_in_dim(value, shard * size, size)

    ff, qw, kw = z.ff, z.qw, z.kw
    return (
        layer_out[None],
        tokens_grad[None],
        mine_of(small[:width], own),
        query_g,
        kv_g[:, :kw],
        kv_g[:, kw:],
        out_g.T,
        mine_of(small[2 * width : 2 * width + HEAD_SIZE], qk),
        mine_of(small[2 * width + HEAD_SIZE :], qk),
        mine_of(small[width : 2 * width], own),
        gu_g[:, :ff],
        gu_g[:, ff:],
        down_g.T,
    )


def solution(mesh):
    placed = (
        P("shard", "ctx", None),
        P("shard", "ctx", None),
        P(),
        P("shard"),
        P("shard", "tp"),
        P("shard", "tp"),
        P("shard", "tp"),
        P("tp", "shard"),
        P("shard"),
        P("shard"),
        P("shard"),
        P("shard", "tp"),
        P("shard", "tp"),
        P("tp", "shard"),
    )
    return jax.shard_map(
        per_device,
        mesh=mesh,
        in_specs=placed,
        out_specs=(
            P("shard", "ctx", None),
            P("shard", "ctx", None),
            P("shard"),
            P("shard", "tp"),
            P("shard", "tp"),
            P("shard", "tp"),
            P("tp", "shard"),
            P("shard"),
            P("shard"),
            P("shard"),
            P("shard", "tp"),
            P("shard", "tp"),
            P("tp", "shard"),
        ),
        check_vma=False,
    )
```
